128 devices in a mesh: row: 8 (over z, x_lo), col: 16 (over x_hi, y, core).
Axes of the slice: x: 4 (x_hi: 2, x_lo: 2; x = x_hi * 2 + x_lo), y: 4, z: 4, core: 2. Of those that a mesh axis runs over, the one named last changes fastest.
Arguments:
- right_side: float32 [3, 24576], P(None, ('row', 'col'))
- linewidth: float32 [24576], P(('row', 'col')), may hold values from 0.6 to 2.4
- scattering: float32 [24576, 24576], P('row', 'col'), as said below
Outputs:
- solution: float32 [3, 24576], P(None, ('row', 'col'))
- residual: float32 [3, 24576], P(None, ('row', 'col'))
The draws below stay inside these ranges and needn't reach their ends.
Inputs may be any that keep to these rules, and one draw needn't show every extreme that they name: scattering is symmetric.
All inputs are finite; a program needn't handle non-finite values.
Results may differ from the reference program's by a relative error of at most 0.00018.
Values sent between devices are 32-bit elements; how exact they have to be, the bound alone decides.
A program may use at most 64 MiB of HBM per device.

```python
import math
import jax
import jax.numpy as jnp
from jax import lax

MODES = 24576
COMPONENTS = 3
ITERS = 2


def draw_scattering(key, part):
    base = jax.random.normal(key, (MODES, MODES), jnp.float32)
    return (base + base.T) * (0.2 / math.sqrt(2.0 * MODES))


def draw_right_side(key, part):
    position = jnp.arange(MODES, dtype=jnp.float32) / (MODES - 1)
    values = jax.random.normal(key, (COMPONENTS, MODES), jnp.float32)
    return values * jnp.exp(math.log(3.0) * position)[None, :]


def block_levels(rng, extent, shards, smallest, top_value):
    def one(axis_at, blocks):
        heights = jax.random.uniform(jax.random.fold_in(jax.random.fold_in(rng, 6), axis_at), (blocks,), jnp.float32, smallest / len(shards), top_value / len(shards))
        return jnp.repeat(jnp.exp(heights), extent[axis_at] // blocks).reshape((-1,) + (1,) * (len(extent) - axis_at - 1))

    gain = one(*shards[0])
    for cut in shards[1:]:
        gain = gain * one(*cut)
    return gain


def setup_inputs(seed: int = 0) -> dict:
    splits = jax.random.split(jax.random.key(seed), 4)
    return {
        "right_side": draw_right_side(jax.random.fold_in(splits[3], 71), 0),
        "linewidth": jnp.clip(jnp.exp(math.log(2.4) - 1.3862944 * jax.random.uniform(splits[1], (MODES,), jnp.float32) ** block_levels(splits[1], (MODES,), ((0, 128),), -0.2, 0.2)), 0.6, 2.4),
        "scattering": draw_scattering(jax.random.fold_in(splits[3], 71), 0),
    }


def apply_operator(vectors, linewidth, scattering):
    product = lax.dot_general(vectors, scattering, (((1,), (1,)), ((), ())), precision=lax.Precision.HIGHEST, preferred_element_type=jnp.float32)
    return linewidth[None, :] * vectors + product


def reference(right_side, linewidth, scattering):
    solution = jnp.zeros_like(right_side)
    residual = right_side
    direction = right_side
    norm_now = jnp.sum(residual * residual, axis=1)
    for iteration in range(ITERS):
        image = apply_operator(direction, linewidth, scattering)
        step_size = norm_now / jnp.sum(direction * image, axis=1)
        solution = solution + step_size[:, None] * direction
        residual = residual - step_size[:, None] * image
        norm_next = jnp.sum(residual * residual, axis=1)
        direction = residual + (norm_next / norm_now)[:, None] * direction
        norm_now = norm_next
    return solution, residual
```

```python
import functools

import jax
import jax.numpy as jnp
from jax import lax
from jax.experimental import pallas as pl
from jax.experimental.pallas import tpu as pltpu
from jax.sharding import PartitionSpec as P

ROW_COL = ("row", "col")
MESH = pl.DeviceIdType.MESH
F32, BF16 = jnp.float32, jnp.bfloat16
PAD = 256


def three_parts(rows):
    top = rows.astype(BF16).astype(F32)
    rest = rows - top
    middle = rest.astype(BF16).astype(F32)
    low = rest - middle
    return jnp.concatenate([top, middle, low, jnp.zeros_like(low)], axis=0).astype(BF16)


def joined(product):
    return product[0:4] + product[4:8] + product[8:12]


def await_bytes(ref, count, sem):
    part = ref.at[pl.ds(0, count)]
    pltpu.make_async_copy(part, part, sem).wait()


def kernel(rows_n, cols_n, b_ref, width_ref, s_hbm, x_ref, res_ref,
           s_f32, s_hi, s_lo, a_slot, v_buf, p_slot, w_buf, own_w, q_buf, d_slot, e_slot,
           s_sem, send_sem, recv_sem, own_sem):
    row, col = lax.axis_index("row"), lax.axis_index("col")
    me = row * cols_n + col
    block_rows, block_cols = s_f32.shape
    modes = b_ref.shape[1]
    chunk = modes
    chunks = block_rows // chunk
    odd = lax.rem(col, 2)

    def load(i):
        at = pl.ds(pl.multiple_of(i * chunk, chunk), chunk)
        return pltpu.make_async_copy(s_hbm.at[at], s_f32.at[at], s_sem.at[i])

    def start_load(i, _):
        load(i).start()
        return 0

    lax.fori_loop(0, chunks, start_load, 0)

    row_peers = [(row, lax.rem(col + i, cols_n)) for i in range(1, cols_n)]
    col_peers = [(lax.rem(row + i, rows_n), col) for i in range(1, rows_n)]
    barrier = pltpu.get_barrier_semaphore()
    for peer in row_peers + col_peers:
        pl.semaphore_signal(barrier, inc=1, device_id=peer, device_id_type=MESH)

    lanes = lax.broadcasted_iota(jnp.int32, (4, PAD), 1)
    shift = odd * (PAD - modes)
    mine = (lanes >= shift) & (lanes < shift + modes)
    fresh = jnp.concatenate([b_ref[...], width_ref[...]], axis=0)
    fresh = jnp.concatenate([fresh, jnp.zeros((4, PAD - modes), F32)], axis=1)
    own_b = jnp.where(odd == 1, pltpu.roll(fresh, PAD - modes, 1), fresh)
    a_slot[col] = own_b
    pl.semaphore_wait(barrier, rows_n + cols_n - 2)

    def send(src, dst, peer, at):
        copy = pltpu.make_async_remote_copy(
            src_ref=src, dst_ref=dst, send_sem=send_sem.at[at], recv_sem=recv_sem.at[at],
            device_id=peer, device_id_type=MESH)
        copy.start()

    for peer in row_peers:
        send(a_slot.at[col], a_slot.at[col], peer, 0)

    step = 32

    def split_chunk(i, _):
        load(i).wait()

        def split(k, _):
            at = pl.ds(pl.multiple_of(i * chunk + k * step, step), step)
            whole = s_f32[at]
            high = whole.astype(BF16)
            s_hi[at] = high
            s_lo[at] = (whole - high.astype(F32)).astype(BF16)
            return 0

        return lax.fori_loop(0, chunk // step, split, 0)

    lax.fori_loop(0, chunks, split_chunk, 0)

    await_bytes(a_slot, cols_n - 1, recv_sem.at[0])
    pieces = []
    for pair in range(cols_n // 2):
        left, right = a_slot[2 * pair], a_slot[2 * pair + 1]
        pieces += [left[:, :128], left[:, 128:] + right[:, :128], right[:, 128:]]
    vector = jnp.concatenate(pieces, axis=1)
    v_buf[...] = vector

    depth = 512
    v_parts = three_parts(vector)
    w_in = w_buf
    total = jnp.zeros((16, block_cols), F32)
    for k in range(block_rows // depth):
        part = v_parts[:, k * depth:(k + 1) * depth]
        at = pl.ds(k * depth, depth)
        total = total + jnp.dot(part, s_hi[at], preferred_element_type=F32)
        total = total + jnp.dot(part, s_lo[at], preferred_element_type=F32)
    on_diagonal = row == col // 2
    half = v_buf[:, pl.ds(pl.multiple_of(odd * block_cols, 128), block_cols)]
    flag = jnp.where(on_diagonal, 1.0, 0.0).astype(F32)
    p_slot[row] = joined(total) + half * half[3:4] * flag
    for peer in col_peers:
        send(p_slot.at[row], p_slot.at[row], peer, 1)
    await_bytes(p_slot, rows_n - 1, recv_sem.at[1])
    w1 = p_slot[0]
    for i in range(1, rows_n):
        w1 = w1 + p_slot[i]
    w_in[...] = w1

    per_block = block_cols // modes

    def window(j):
        return pl.ds(pl.multiple_of((j // 2) * (2 * modes) + lax.rem(j, 2) * 128, 128), PAD)

    @pl.when(on_diagonal)
    def _():
        def give(j, _):
            to = odd * per_block + j

            @pl.when(to != col)
            def _():
                pltpu.make_async_remote_copy(
                    src_ref=w_buf.at[:, window(j)], dst_ref=own_w, send_sem=own_sem.at[0], recv_sem=own_sem.at[1],
                    device_id=(row, to), device_id_type=MESH).start()

            @pl.when(to == col)
            def _():
                own_w[...] = w_buf[:, window(j)]

            return 0

        lax.fori_loop(0, per_block, give, 0)

    w_parts = three_parts(w1)
    width = 2 * modes

    def second(i, _):
        at = pl.ds(pl.multiple_of(i * width, width), width)
        dims = (((1,), (1,)), ((), ()))
        out = lax.dot_general(w_parts, s_hi[at], dims, preferred_element_type=F32)
        out = out + lax.dot_general(w_parts, s_lo[at], dims, preferred_element_type=F32)
        q_buf[:, at] = joined(out)
        for j in range(2):
            to = 2 * i + j

            @pl.when(to != col)
            def _():
                send(q_buf.at[:, window(to)], d_slot.at[col], (row, to), 2)

        return 0

    lax.fori_loop(0, block_rows // width, second, 0)
    d_slot[col] = q_buf[:, window(col)]

    giver = 2 * row + col // per_block
    @pl.when(giver != col)
    def _():
        pltpu.make_async_copy(own_w, own_w, own_sem.at[1]).wait()

    await_bytes(d_slot, cols_n - 1, recv_sem.at[2])
    own_w1 = jnp.where(mine, own_w[...], 0.0)
    w2 = d_slot[0]
    for i in range(1, cols_n):
        w2 = w2 + d_slot[i]
    own_w2 = jnp.where(mine, w2, 0.0) + own_b[3:4] * own_w1

    def inner(u, v):
        return jnp.sum(u * v, axis=1, keepdims=True)

    lane = lax.broadcasted_iota(jnp.int32, (4, 128), 1)
    moments = jnp.where(lane == 0, inner(own_b, own_b),
              jnp.where(lane == 1, inner(own_b, own_w1),
              jnp.where(lane == 2, inner(own_w1, own_w1), inner(own_w1, own_w2))))
    e_slot[me] = moments
    n = rows_n * cols_n

    def tell(i, _):
        to = lax.rem(me + i, n)
        send(e_slot.at[me], e_slot.at[me], (to // cols_n, lax.rem(to, cols_n)), 3)
        return 0

    lax.fori_loop(1, n, tell, 0, unroll=8)
    await_bytes(e_slot, n - 1, recv_sem.at[3])
    g = jnp.sum(e_slot[...], axis=0)
    g0, g1, g2, g3 = (g[:, i:i + 1] for i in range(4))
    a0 = g0 / g1
    norm = g0 - 2.0 * a0 * g1 + a0 * a0 * g2
    beta = norm / g0
    more = 1.0 + beta
    a1 = norm / (more * more * g1 - 2.0 * more * a0 * g2 + a0 * a0 * g3)
    r1 = own_b - a0 * own_w1
    x2 = a0 * own_b + a1 * (r1 + beta * own_b)
    r2 = r1 - a1 * (more * own_w1 - a0 * own_w2)
    x2 = jnp.where(odd == 1, pltpu.roll(x2, modes, 1), x2)
    r2 = jnp.where(odd == 1, pltpu.roll(r2, modes, 1), r2)
    x_ref[...] = x2[0:3, :modes]
    res_ref[...] = r2[0:3, :modes]

    await_bytes(a_slot, cols_n - 1, send_sem.at[0])
    await_bytes(p_slot, rows_n - 1, send_sem.at[1])
    await_bytes(d_slot, cols_n - 1, send_sem.at[2])
    await_bytes(e_slot, n - 1, send_sem.at[3])

    @pl.when(on_diagonal)
    def _():
        def sent(j, _):
            @pl.when(odd * per_block + j != col)
            def _():
                pltpu.make_async_copy(own_w, own_w, own_sem.at[0]).wait()

            return 0

        lax.fori_loop(0, per_block, sent, 0)


def solution(mesh):
    rows_n, cols_n = mesh.shape["row"], mesh.shape["col"]
    n = rows_n * cols_n

    def body(right_side, linewidth, scattering):
        block_rows, block_cols = scattering.shape
        vmem = pl.BlockSpec(memory_space=pltpu.VMEM)
        out = jax.ShapeDtypeStruct(right_side.shape, F32)
        return pl.pallas_call(
            functools.partial(kernel, rows_n, cols_n),
            out_shape=(out, out),
            in_specs=[vmem, vmem, pl.BlockSpec(memory_space=pl.ANY)],
            out_specs=(vmem, vmem),
            scratch_shapes=[
                pltpu.VMEM((block_rows, block_cols), F32),
                pltpu.VMEM((block_rows, block_cols), BF16),
                pltpu.VMEM((block_rows, block_cols), BF16),
                pltpu.VMEM((cols_n, 4, PAD), F32),
                pltpu.VMEM((4, block_rows), F32),
                pltpu.VMEM((rows_n, 4, block_cols), F32),
                pltpu.VMEM((4, block_cols), F32),
                pltpu.VMEM((4, PAD), F32),
                pltpu.VMEM((4, block_rows), F32),
                pltpu.VMEM((cols_n, 4, PAD), F32),
                pltpu.VMEM((n, 4, 128), F32),
                pltpu.SemaphoreType.DMA((cols_n,)),
                pltpu.SemaphoreType.DMA((4,)),
                pltpu.SemaphoreType.DMA((4,)),
                pltpu.SemaphoreType.DMA((2,)),
            ],
            compiler_params=pltpu.CompilerParams(
                collective_id=0, has_side_effects=True, vmem_limit_bytes=60 << 20),
        )(right_side, linewidth.reshape(1, -1), scattering)

    return jax.shard_map(
        body,
        mesh=mesh,
        in_specs=(P(None, ROW_COL), P(ROW_COL), P("row", "col")),
        out_specs=(P(None, ROW_COL), P(None, ROW_COL)),
        check_vma=False,
    )
```

```python
import functools

import jax
import jax.numpy as jnp
from jax import lax
from jax.experimental import pallas as pl
from jax.experimental.pallas import tpu as pltpu
from jax.sharding import PartitionSpec as P

ROW_COL = ("row", "col")
MESH = pl.DeviceIdType.MESH
F32, BF16 = jnp.float32, jnp.bfloat16
LANES = 128
PAD = 2 * LANES


def three_parts(rows):
    top = rows.astype(BF16).astype(F32)
    rest = rows - top
    middle = rest.astype(BF16).astype(F32)
    low = rest - middle
    return jnp.concatenate([top, middle, low, jnp.zeros_like(low)], axis=0).astype(BF16)


def joined(product):
    return product[0:4] + product[4:8] + product[8:12]


def await_bytes(ref, count, sem):
    part = ref.at[pl.ds(0, count)]
    pltpu.make_async_copy(part, part, sem).wait()


def ring(d):
    return min(d, 4 - d)


def farthest_first(offsets):
    hops = lambda o: ring(o[0]) + ring(o[1]) + ring(o[2]) + 0.1 * o[3]
    return sorted((o for o in offsets if any(o)), key=lambda o: -hops(o))


def far_fourth(j):
    return 2 - j + 3 * (j // 2) - 2 * ((j + 1) // 4)


def kernel(rows_n, cols_n, b_hbm, width_hbm, s_hbm, x_part, res_part, res_step,
           s_f32, s_hi, s_lo, t_hi, t_lo, b_in, width_in, a_slot, v_buf, p_slot, w_buf, f_slot, q_buf,
           d_slot, e_slot, s_sem, in_sem, a_sem, send_sem, recv_sem):
    row, col = lax.axis_index("row"), lax.axis_index("col")
    me = row * cols_n + col
    block_rows, block_cols = s_f32.shape
    modes = b_in.shape[1]
    chips = cols_n // 2
    width = 2 * modes
    odd = col % 2

    z, x_lo, x_hi, y = row // 2, row % 2, col // 8, (col // 2) % 4
    x = x_hi * 2 + x_lo
    z_at = [((z + d) % 4) * 2 for d in range(4)]
    y_at = [((y + d) % 4) * 2 for d in range(4)]
    x_row = [((x + d) % 4) % 2 for d in range(4)]
    x_col = [((x + d) % 4) // 2 * 8 for d in range(4)]
    core_at = [odd, 1 - odd]

    def device(offset):
        dz, dy, dx, dc = offset
        return (z_at[dz] + x_row[dx], x_col[dx] + y_at[dy] + core_at[dc])

    def col_device(offset):
        dz, _, dx, _ = offset
        return (z_at[dz] + (row + dx) % 2, col)

    row_peers = [device(o) for o in farthest_first([(0, dy, dx, dc) for dy in range(4) for dx in (0, 2) for dc in (0, 1)])]
    col_peers = [col_device(o) for o in farthest_first([(dz, 0, dx, 0) for dz in range(4) for dx in (0, 1)])]
    everyone = [device(o) for o in farthest_first(
        [(dz, dy, dx, dc) for dz in range(4) for dy in range(4) for dx in range(4) for dc in (0, 1)])]

    small = [pltpu.make_async_copy(b_hbm, b_in, in_sem.at[0]), pltpu.make_async_copy(width_hbm, width_in, in_sem.at[1])]
    for copy in small:
        copy.start()
    barrier = pltpu.get_barrier_semaphore()
    for peer in row_peers + col_peers:
        pl.semaphore_signal(barrier, inc=1, device_id=peer, device_id_type=MESH)

    def near_chip(i):
        return ((x_hi + i // 4) % 2) * 4 + (y + far_fourth(3 - i % 4)) % 4

    def chip_rows(i):
        return pl.ds(pl.multiple_of(near_chip(i) * width, width), width)

    def load(i):
        at = chip_rows(i)
        return pltpu.make_async_copy(s_hbm.at[at], s_f32.at[at], s_sem.at[i])

    def start_load(i, _):
        load(i).start()
        return 0

    lax.fori_loop(0, chips, start_load, 0)

    for copy in small:
        copy.wait()
    lanes = lax.broadcasted_iota(jnp.int32, (4, PAD), 1)
    shift = odd * (PAD - modes)
    mine = (lanes >= shift) & (lanes < shift + modes)
    fresh = jnp.concatenate([b_in[...], width_in[...]], axis=0)
    fresh = jnp.concatenate([fresh, jnp.zeros((4, PAD - modes), F32)], axis=1)
    own_b = jnp.where(odd == 1, pltpu.roll(fresh, PAD - modes, 1), fresh)
    a_slot[col] = own_b
    pl.semaphore_wait(barrier, rows_n + cols_n - 2)

    def send(src, dst, peer, at, arrived=None):
        copy = pltpu.make_async_remote_copy(
            src_ref=src, dst_ref=dst, send_sem=send_sem.at[at],
            recv_sem=recv_sem.at[at] if arrived is None else arrived,
            device_id=peer, device_id_type=MESH)
        copy.start()

    for peer in row_peers:
        send(a_slot.at[col], a_slot.at[col], peer, 0, a_sem.at[col])

    def split(i):
        load(i).wait()

        def some(k, _):
            at = pl.ds(pl.multiple_of(near_chip(i) * width + k * 64, 64), 64)
            whole = s_f32[at]
            high = whole.astype(BF16)
            s_hi[at] = high
            s_lo[at] = (whole - high.astype(F32)).astype(BF16)
            return 0

        lax.fori_loop(0, width // 64, some, 0)

    def turn(i):
        def some(k, _):
            at = pl.ds(pl.multiple_of(near_chip(i) * width + k * LANES, LANES), LANES)
            t_hi[:, at] = s_hi[at].T
            t_lo[:, at] = s_lo[at].T
            return 0

        lax.fori_loop(0, width // LANES, some, 0)

    early = chips // 2

    def prepare(i, _):
        split(i)
        turn(i)
        return 0

    lax.fori_loop(0, early, prepare, 0)

    def first(i, total):
        @pl.when(i >= early)
        def _():
            split(i)

        chip = near_chip(i)
        for j in range(2):
            @pl.when(2 * chip + j != col)
            def _():
                arrived = a_slot.at[2 * chip + j]
                pltpu.make_async_copy(arrived, arrived, a_sem.at[2 * chip + j]).wait()

        left, right = a_slot[2 * chip], a_slot[2 * chip + 1]
        vector = jnp.concatenate([left[:, :LANES], left[:, LANES:] + right[:, :LANES], right[:, LANES:]], axis=1)
        at = chip_rows(i)
        v_buf[:, at] = vector
        part = three_parts(vector)
        total = total + jnp.dot(part, s_hi[at], preferred_element_type=F32)
        return total + jnp.dot(part, s_lo[at], preferred_element_type=F32)

    total = lax.fori_loop(0, chips, first, jnp.zeros((16, block_cols), F32))
    on_diagonal = row == col // 2
    half = v_buf[:, pl.ds(pl.multiple_of(odd * block_cols, LANES), block_cols)]
    flag = jnp.where(on_diagonal, 1.0, 0.0).astype(F32)
    p_slot[row] = joined(total) + half * half[3:4] * flag
    for peer in col_peers:
        send(p_slot.at[row], p_slot.at[row], peer, 1)

    def turn_late(i, _):
        turn(i)
        return 0

    lax.fori_loop(early, chips, turn_late, 0)
    await_bytes(p_slot, rows_n - 1, recv_sem.at[1])
    w1 = p_slot[0]
    for i in range(1, rows_n):
        w1 = w1 + p_slot[i]
    w_buf[...] = w1

    home = col // 2
    away = (z - home // 2) % 4
    across = jnp.where(x_lo == home % 2, 0, 1)
    giving = away < 2
    targets = []
    for j in range(2):
        y_to = (y + jnp.where(away == 0, 2 - j, 3 * j)) % 4
        targets += [(home, ((x_hi + across) % 2) * 8 + y_to * 2 + core) for core in range(2)]

    @pl.when(giving)
    def _():
        for peer in targets:
            send(w_buf, f_slot.at[odd], peer, 2)

    def window(j):
        return pl.ds(pl.multiple_of((j // 2) * width + (j % 2) * LANES, LANES), PAD)

    w_parts = three_parts(w1)
    for i in range(cols_n // 4):
        at = pl.ds(i * 2 * width, 2 * width)
        out = jnp.dot(w_parts, t_hi[:, at], preferred_element_type=F32)
        out = out + jnp.dot(w_parts, t_lo[:, at], preferred_element_type=F32)
        q_buf[:, at] = joined(out)
        for j in range(4):
            to = 4 * i + j

            @pl.when(to != col)
            def _():
                send(q_buf.at[:, window(to)], d_slot.at[col], (row, to), 3)

    d_slot[col] = q_buf[:, window(col)]

    await_bytes(f_slot, 2, recv_sem.at[2])
    per_block = block_cols // modes
    own_w1 = jnp.where(mine, f_slot[col // per_block, :, window(col % per_block)], 0.0)

    def inner(u, v):
        return jnp.sum(u * v, axis=1, keepdims=True)

    cross = jnp.zeros((4, LANES), F32)
    per_half = block_cols // LANES
    for i in range(block_rows // LANES):
        near = f_slot[i // per_half, :, (i % per_half) * LANES:(i % per_half + 1) * LANES]
        cross = cross + near * q_buf[:, i * LANES:(i + 1) * LANES]
    last = jnp.sum(cross, axis=1, keepdims=True) + inner(own_b[3:4] * own_w1, own_w1)
    lane = lax.broadcasted_iota(jnp.int32, (4, LANES), 1)
    table = jnp.zeros((4, LANES), F32)
    for i, moment in enumerate([inner(own_b, own_b), inner(own_b, own_w1), inner(own_w1, own_w1), last]):
        table = jnp.where(lane == i, moment, table)
    line = table[0:1] + pltpu.roll(table[1:2], 4, 1) + pltpu.roll(table[2:3], 8, 1)
    e_slot[pl.ds(me, 1)] = line
    for peer in everyone:
        send(e_slot.at[pl.ds(me, 1)], e_slot.at[pl.ds(me, 1)], peer, 4)

    await_bytes(d_slot, cols_n - 1, recv_sem.at[3])
    w2 = d_slot[0]
    for i in range(1, cols_n):
        w2 = w2 + d_slot[i]
    own_w2 = jnp.where(mine, w2, 0.0) + own_b[3:4] * own_w1

    n = rows_n * cols_n
    await_bytes(e_slot, n - 1, recv_sem.at[4])
    line = jnp.sum(e_slot[...], axis=0, keepdims=True)
    g = jnp.concatenate([line, pltpu.roll(line, LANES - 4, 1), pltpu.roll(line, LANES - 8, 1), line], axis=0)
    g0, g1, g2, g3 = (g[:, i:i + 1] for i in range(4))
    a0 = g0 / g1
    norm = g0 - 2.0 * a0 * g1 + a0 * a0 * g2
    beta = norm / g0
    more = 1.0 + beta
    a1 = norm / (more * more * g1 - 2.0 * more * a0 * g2 + a0 * a0 * g3)
    r1 = own_b - a0 * own_w1
    results = [a0 * own_b + a1 * (r1 + beta * own_b) - r1, r1, a1 * (more * own_w1 - a0 * own_w2)]
    for ref, value in zip((x_part, res_part, res_step), results):
        value = jnp.where(odd == 1, pltpu.roll(value, modes, 1), value)
        ref[...] = value[0:3, :modes]

    await_bytes(a_slot, cols_n - 1, send_sem.at[0])
    await_bytes(p_slot, rows_n - 1, send_sem.at[1])
    await_bytes(d_slot, cols_n - 1, send_sem.at[3])
    await_bytes(e_slot, n - 1, send_sem.at[4])

    @pl.when(giving)
    def _():
        await_bytes(f_slot, 2, send_sem.at[2])
        await_bytes(f_slot, 2, send_sem.at[2])


def solution(mesh):
    rows_n, cols_n = mesh.shape["row"], mesh.shape["col"]
    n = rows_n * cols_n

    def body(right_side, linewidth, scattering):
        block_rows, block_cols = scattering.shape
        vmem, anywhere = pl.BlockSpec(memory_space=pltpu.VMEM), pl.BlockSpec(memory_space=pl.ANY)
        line = linewidth.reshape(1, -1)
        x_part, res_part, res_step = pl.pallas_call(
            functools.partial(kernel, rows_n, cols_n),
            out_shape=(pltpu.VMEM(right_side.shape, F32),) * 3,
            in_specs=[anywhere] * 3,
            out_specs=(vmem,) * 3,
            scratch_shapes=[
                pltpu.VMEM((block_rows, block_cols), F32),
                pltpu.VMEM((block_rows, block_cols), BF16),
                pltpu.VMEM((block_rows, block_cols), BF16),
                pltpu.VMEM((block_cols, block_rows), BF16),
                pltpu.VMEM((block_cols, block_rows), BF16),
                pltpu.VMEM(right_side.shape, F32),
                pltpu.VMEM(line.shape, F32),
                pltpu.VMEM((cols_n, 4, PAD), F32),
                pltpu.VMEM((4, block_rows), F32),
                pltpu.VMEM((rows_n, 4, block_cols), F32),
                pltpu.VMEM((4, block_cols), F32),
                pltpu.VMEM((2, 4, block_cols), F32),
                pltpu.VMEM((4, block_rows), F32),
                pltpu.VMEM((cols_n, 4, PAD), F32),
                pltpu.VMEM((n, LANES), F32),
                pltpu.SemaphoreType.DMA((cols_n // 2,)),
                pltpu.SemaphoreType.DMA((2,)),
                pltpu.SemaphoreType.DMA((cols_n,)),
                pltpu.SemaphoreType.DMA((5,)),
                pltpu.SemaphoreType.DMA((5,)),
            ],
            compiler_params=pltpu.CompilerParams(
                collective_id=0, has_side_effects=True, vmem_limit_bytes=60 << 20),
        )(right_side, line, scattering)
        return x_part + res_part, res_part - res_step

    return jax.shard_map(
        body,
        mesh=mesh,
        in_specs=(P(None, ROW_COL), P(ROW_COL), P("row", "col")),
        out_specs=(P(None, ROW_COL), P(None, ROW_COL)),
        check_vma=False,
    )
```

```python
import functools

import jax
import jax.numpy as jnp
from jax import lax
from jax.experimental import pallas as pl
from jax.experimental.pallas import tpu as pltpu
from jax.sharding import PartitionSpec as P

ROW_COL = ("row", "col")
MESH = pl.DeviceIdType.MESH
F32, BF16 = jnp.float32, jnp.bfloat16
LANES = 128
TURNED = 5
FAR = 44
PAD = 2 * LANES


def three_parts(rows):
    top = rows.astype(BF16).astype(F32)
    rest = rows - top
    middle = rest.astype(BF16).astype(F32)
    low = rest - middle
    return jnp.concatenate([top, middle, low, jnp.zeros_like(low)], axis=0).astype(BF16)


def joined(product):
    return product[0:4] + product[4:8] + product[8:12]


def await_bytes(ref, count, sem):
    part = ref.at[pl.ds(0, count)]
    pltpu.make_async_copy(part, part, sem).wait()


def ring(d):
    return min(d, 4 - d)


def farthest_first(offsets):
    hops = lambda o: ring(o[0]) + ring(o[1]) + ring(o[2]) + 0.1 * o[3]
    return sorted((o for o in offsets if any(o)), key=lambda o: -hops(o))


def far_fourth(j):
    return 2 - j + 3 * (j // 2) - 2 * ((j + 1) // 4)


def kernel(rows_n, cols_n, b_hbm, width_hbm, s_hbm, x_part, res_part, res_step,
           s_f32, s_hi, s_lo, t_hi, t_lo, b_in, width_in, a_slot, v_buf, p_slot, w_buf, f_slot, q_buf,
           d_slot, e_slot, s_sem, in_sem, a_sem, send_sem, recv_sem):
    row, col = lax.axis_index("row"), lax.axis_index("col")
    me = row * cols_n + col
    block_rows, block_cols = s_f32.shape
    modes = b_in.shape[1]
    chips = cols_n // 2
    width = 2 * modes
    odd = col % 2

    z, x_lo, x_hi, y = row // 2, row % 2, col // 8, (col // 2) % 4
    x = x_hi * 2 + x_lo
    z_at = [((z + d) % 4) * 2 for d in range(4)]
    y_at = [((y + d) % 4) * 2 for d in range(4)]
    x_row = [((x + d) % 4) % 2 for d in range(4)]
    x_col = [((x + d) % 4) // 2 * 8 for d in range(4)]
    core_at = [odd, 1 - odd]

    def device(offset):
        dz, dy, dx, dc = offset
        return (z_at[dz] + x_row[dx], x_col[dx] + y_at[dy] + core_at[dc])

    def col_device(offset):
        dz, _, dx, _ = offset
        return (z_at[dz] + (row + dx) % 2, col)

    row_peers = [device(o) for o in farthest_first([(0, dy, dx, dc) for dy in range(4) for dx in (0, 2) for dc in (0, 1)])]
    col_peers = [col_device(o) for o in farthest_first([(dz, 0, dx, 0) for dz in range(4) for dx in (0, 1)])]
    everyone = [device(o) for o in farthest_first(
        [(dz, dy, dx, dc) for dz in range(4) for dy in range(4) for dx in range(4) for dc in (0, 1)])]

    small = [pltpu.make_async_copy(b_hbm, b_in, in_sem.at[0]), pltpu.make_async_copy(width_hbm, width_in, in_sem.at[1])]
    for copy in small:
        copy.start()
    barrier = pltpu.get_barrier_semaphore()
    for peer in row_peers + col_peers:
        pl.semaphore_signal(barrier, inc=1, device_id=peer, device_id_type=MESH)

    def near_chip(i):
        return ((x_hi + i // 4) % 2) * 4 + (y + far_fourth(3 - i % 4)) % 4

    def chip_rows(i):
        return pl.ds(pl.multiple_of(near_chip(i) * width, width), width)

    def load(i):
        at = chip_rows(i)
        return pltpu.make_async_copy(s_hbm.at[at], s_f32.at[at], s_sem.at[i])

    def start_load(i, _):
        load(i).start()
        return 0

    lax.fori_loop(0, chips, start_load, 0)

    for copy in small:
        copy.wait()
    lanes = lax.broadcasted_iota(jnp.int32, (4, PAD), 1)
    shift = odd * (PAD - modes)
    mine = (lanes >= shift) & (lanes < shift + modes)
    fresh = jnp.concatenate([b_in[...], width_in[...]], axis=0)
    fresh = jnp.concatenate([fresh, jnp.zeros((4, PAD - modes), F32)], axis=1)
    own_b = jnp.where(odd == 1, pltpu.roll(fresh, PAD - modes, 1), fresh)
    a_slot[col] = own_b
    pl.semaphore_wait(barrier, rows_n + cols_n - 2)

    def send(src, dst, peer, at, arrived=None):
        copy = pltpu.make_async_remote_copy(
            src_ref=src, dst_ref=dst, send_sem=send_sem.at[at],
            recv_sem=recv_sem.at[at] if arrived is None else arrived,
            device_id=peer, device_id_type=MESH)
        copy.start()

    for peer in row_peers:
        send(a_slot.at[col], a_slot.at[col], peer, 0, a_sem.at[col])

    def split(i):
        load(i).wait()

        def some(k, _):
            at = pl.ds(pl.multiple_of(near_chip(i) * width + k * 64, 64), 64)
            whole = s_f32[at]
            high = whole.astype(BF16)
            s_hi[at] = high
            s_lo[at] = (whole - high.astype(F32)).astype(BF16)
            return 0

        lax.fori_loop(0, width // 64, some, 0)

    early = chips // 2

    def prepare(i, _):
        split(i)
        return 0

    lax.fori_loop(0, early, prepare, 0)

    total = jnp.zeros((16, block_cols), F32)
    for i in range(chips):
        if i >= early:
            split(i)
        chip = near_chip(i)
        for j in range(2):
            @pl.when(2 * chip + j != col)
            def _():
                arrived = a_slot.at[2 * chip + j]
                pltpu.make_async_copy(arrived, arrived, a_sem.at[2 * chip + j]).wait()

        left, right = a_slot[2 * chip], a_slot[2 * chip + 1]
        vector = jnp.concatenate([left[:, :LANES], left[:, LANES:] + right[:, :LANES], right[:, LANES:]], axis=1)
        at = chip_rows(i)
        v_buf[:, at] = vector
        part = three_parts(vector)
        total = total + jnp.dot(part, s_hi[at], preferred_element_type=F32)
        total = total + jnp.dot(part, s_lo[at], preferred_element_type=F32)
    on_diagonal = row == col // 2
    half = v_buf[:, pl.ds(pl.multiple_of(odd * block_cols, LANES), block_cols)]
    flag = jnp.where(on_diagonal, 1.0, 0.0).astype(F32)
    p_slot[row] = joined(total) + half * half[3:4] * flag
    for peer in col_peers:
        send(p_slot.at[row], p_slot.at[row], peer, 1)

    turned = t_hi.shape[1]
    per_chip = width // LANES

    def turn(i, _):
        rows = pl.ds(pl.multiple_of(near_chip(i // per_chip) * width + (i % per_chip) * LANES, LANES), LANES)
        at = pl.ds(pl.multiple_of(i * LANES, LANES), LANES)
        t_hi[:, at] = s_hi[rows].T
        t_lo[:, at] = s_lo[rows].T
        return 0

    lax.fori_loop(0, turned // LANES, turn, 0)
    await_bytes(p_slot, rows_n - 1, recv_sem.at[1])
    w1 = p_slot[0]
    for i in range(1, rows_n):
        w1 = w1 + p_slot[i]
    w_buf[...] = w1

    home = col // 2
    away = (z - home // 2) % 4
    across = jnp.where(x_lo == home % 2, 0, 1)
    giving = away < 2
    targets = []
    for j in range(2):
        y_to = (y + jnp.where(away == 0, 2 - j, 3 * j)) % 4
        targets += [(home, ((x_hi + across) % 2) * 8 + y_to * 2 + core) for core in range(2)]

    @pl.when(giving)
    def _():
        for peer in targets:
            send(w_buf, f_slot.at[odd], peer, 2)

    def window(j):
        return pl.ds(pl.multiple_of((j // 2) * width + (j % 2) * LANES, LANES), PAD)

    w_parts = three_parts(w1)
    near = jnp.dot(w_parts, t_hi[...], preferred_element_type=F32)
    near = joined(near + jnp.dot(w_parts, t_lo[...], preferred_element_type=F32))
    for i in range(chips):
        at = chip_rows(i)
        if (i + 1) * width <= turned:
            q_buf[:, at] = near[:, i * width:(i + 1) * width]
        else:
            dims = (((1,), (1,)), ((), ()))
            out = lax.dot_general(w_parts, s_hi[at], dims, preferred_element_type=F32)
            q_buf[:, at] = joined(out + lax.dot_general(w_parts, s_lo[at], dims, preferred_element_type=F32))
    d_slot[col] = q_buf[:, window(col)]

    await_bytes(f_slot, 2, recv_sem.at[2])
    per_block = block_cols // modes
    own_w1 = jnp.where(mine, f_slot[col // per_block, :, window(col % per_block)], 0.0)

    def inner(u, v):
        return jnp.sum(u * v, axis=1, keepdims=True)

    cross = jnp.zeros((4, LANES), F32)
    per_half = block_cols // LANES
    for i in range(block_rows // LANES):
        part = f_slot[i // per_half, :, (i % per_half) * LANES:(i % per_half + 1) * LANES]
        cross = cross + part * q_buf[:, i * LANES:(i + 1) * LANES]
    last = jnp.sum(cross, axis=1, keepdims=True) + inner(own_b[3:4] * own_w1, own_w1)
    lane = lax.broadcasted_iota(jnp.int32, (4, LANES), 1)
    table = jnp.zeros((4, LANES), F32)
    for i, moment in enumerate([inner(own_b, own_b), inner(own_b, own_w1), inner(own_w1, own_w1), last]):
        table = jnp.where(lane == i, moment, table)
    line = table[0:1] + pltpu.roll(table[1:2], 4, 1) + pltpu.roll(table[2:3], 8, 1)
    e_slot[pl.ds(me, 1)] = line

    def tell(peers):
        for peer in peers:
            send(e_slot.at[pl.ds(me, 1)], e_slot.at[pl.ds(me, 1)], peer, 4)

    tell(everyone[:FAR])
    for to_row, to_col in row_peers:
        send(q_buf.at[:, window(to_col)], d_slot.at[col], (to_row, to_col), 3)
    tell(everyone[FAR:])

    await_bytes(d_slot, cols_n - 1, recv_sem.at[3])
    w2 = d_slot[0]
    for i in range(1, cols_n):
        w2 = w2 + d_slot[i]
    own_w2 = jnp.where(mine, w2, 0.0) + own_b[3:4] * own_w1

    n = rows_n * cols_n
    await_bytes(e_slot, n - 1, recv_sem.at[4])
    line = jnp.sum(e_slot[...], axis=0, keepdims=True)
    g = jnp.concatenate([line, pltpu.roll(line, LANES - 4, 1), pltpu.roll(line, LANES - 8, 1), line], axis=0)
    g0, g1, g2, g3 = (g[:, i:i + 1] for i in range(4))
    a0 = g0 / g1
    norm = g0 - 2.0 * a0 * g1 + a0 * a0 * g2
    beta = norm / g0
    more = 1.0 + beta
    a1 = norm / (more * more * g1 - 2.0 * more * a0 * g2 + a0 * a0 * g3)
    r1 = own_b - a0 * own_w1
    results = [a0 * own_b + a1 * (r1 + beta * own_b) - r1, r1, a1 * (more * own_w1 - a0 * own_w2)]
    for ref, value in zip((x_part, res_part, res_step), results):
        value = jnp.where(odd == 1, pltpu.roll(value, modes, 1), value)
        ref[...] = value[0:3, :modes]

    await_bytes(a_slot, cols_n - 1, send_sem.at[0])
    await_bytes(p_slot, rows_n - 1, send_sem.at[1])
    await_bytes(d_slot, cols_n - 1, send_sem.at[3])
    await_bytes(e_slot, n - 1, send_sem.at[4])

    @pl.when(giving)
    def _():
        await_bytes(f_slot, 2, send_sem.at[2])
        await_bytes(f_slot, 2, send_sem.at[2])


def solution(mesh):
    rows_n, cols_n = mesh.shape["row"], mesh.shape["col"]
    n = rows_n * cols_n

    def body(right_side, linewidth, scattering):
        block_rows, block_cols = scattering.shape
        vmem, anywhere = pl.BlockSpec(memory_space=pltpu.VMEM), pl.BlockSpec(memory_space=pl.ANY)
        line = linewidth.reshape(1, -1)
        x_part, res_part, res_step = pl.pallas_call(
            functools.partial(kernel, rows_n, cols_n),
            out_shape=(pltpu.VMEM(right_side.shape, F32),) * 3,
            in_specs=[anywhere] * 3,
            out_specs=(vmem,) * 3,
            scratch_shapes=[
                pltpu.VMEM((block_rows, block_cols), F32),
                pltpu.VMEM((block_rows, block_cols), BF16),
                pltpu.VMEM((block_rows, block_cols), BF16),
                pltpu.VMEM((block_cols, block_rows // 8 * TURNED), BF16),
                pltpu.VMEM((block_cols, block_rows // 8 * TURNED), BF16),
                pltpu.VMEM(right_side.shape, F32),
                pltpu.VMEM(line.shape, F32),
                pltpu.VMEM((cols_n, 4, PAD), F32),
                pltpu.VMEM((4, block_rows), F32),
                pltpu.VMEM((rows_n, 4, block_cols), F32),
                pltpu.VMEM((4, block_cols), F32),
                pltpu.VMEM((2, 4, block_cols), F32),
                pltpu.VMEM((4, block_rows), F32),
                pltpu.VMEM((cols_n, 4, PAD), F32),
                pltpu.VMEM((n, LANES), F32),
                pltpu.SemaphoreType.DMA((cols_n // 2,)),
                pltpu.SemaphoreType.DMA((2,)),
                pltpu.SemaphoreType.DMA((cols_n,)),
                pltpu.SemaphoreType.DMA((5,)),
                pltpu.SemaphoreType.DMA((5,)),
            ],
            compiler_params=pltpu.CompilerParams(
                collective_id=0, has_side_effects=True, vmem_limit_bytes=60 << 20),
        )(right_side, line, scattering)
        return x_part + res_part, res_part - res_step

    return jax.shard_map(
        body,
        mesh=mesh,
        in_specs=(P(None, ROW_COL), P(ROW_COL), P("row", "col")),
        out_specs=(P(None, ROW_COL), P(None, ROW_COL)),
        check_vma=False,
    )
```

```python
import functools

import jax
import jax.numpy as jnp
from jax import lax
from jax.experimental import pallas as pl
from jax.experimental.pallas import tpu as pltpu
from jax.sharding import PartitionSpec as P

ROW_COL = ("row", "col")
MESH = pl.DeviceIdType.MESH
F32, BF16 = jnp.float32, jnp.bfloat16
LANES = 128
TURNED = 5
FAR = 44
PAD = 2 * LANES


def three_parts(rows):
    top = rows.astype(BF16).astype(F32)
    rest = rows - top
    middle = rest.astype(BF16).astype(F32)
    low = rest - middle
    return jnp.concatenate([top, middle, low, jnp.zeros_like(low)], axis=0).astype(BF16)


def joined(product):
    return product[0:4] + product[4:8] + product[8:12]


def await_bytes(ref, count, sem):
    part = ref.at[pl.ds(0, count)]
    pltpu.make_async_copy(part, part, sem).wait()


def ring(d):
    return min(d, 4 - d)


def farthest_first(offsets):
    hops = lambda o: ring(o[0]) + ring(o[1]) + ring(o[2]) + 0.1 * o[3]
    return sorted((o for o in offsets if any(o)), key=lambda o: -hops(o))


def far_fourth(j):
    return 2 - j + 3 * (j // 2) - 2 * ((j + 1) // 4)


def kernel(rows_n, cols_n, b_hbm, width_hbm, s_hbm, x_part, res_part, res_step,
           s_f32, s_hi, s_lo, t_hi, t_lo, b_in, width_in, a_slot, v_buf, p_slot, w_buf, f_slot, q_buf,
           d_slot, e_slot, s_sem, in_sem, a_sem, send_sem, recv_sem):
    row, col = lax.axis_index("row"), lax.axis_index("col")
    me = row * cols_n + col
    block_rows, block_cols = s_f32.shape
    modes = b_in.shape[1]
    chips = cols_n // 2
    width = 2 * modes
    odd = col % 2

    z, x_lo, x_hi, y = row // 2, row % 2, col // 8, (col // 2) % 4
    x = x_hi * 2 + x_lo
    z_at = [((z + d) % 4) * 2 for d in range(4)]
    y_at = [((y + d) % 4) * 2 for d in range(4)]
    x_row = [((x + d) % 4) % 2 for d in range(4)]
    x_col = [((x + d) % 4) // 2 * 8 for d in range(4)]
    core_at = [odd, 1 - odd]

    def device(offset):
        dz, dy, dx, dc = offset
        return (z_at[dz] + x_row[dx], x_col[dx] + y_at[dy] + core_at[dc])

    def col_device(offset):
        dz, _, dx, _ = offset
        return (z_at[dz] + (row + dx) % 2, col)

    row_peers = [device(o) for o in farthest_first([(0, dy, dx, dc) for dy in range(4) for dx in (0, 2) for dc in (0, 1)])]
    col_peers = [col_device(o) for o in farthest_first([(dz, 0, dx, 0) for dz in range(4) for dx in (0, 1)])]
    everyone = [device(o) for o in farthest_first(
        [(dz, dy, dx, dc) for dz in range(4) for dy in range(4) for dx in range(4) for dc in (0, 1)])]

    small = [pltpu.make_async_copy(b_hbm, b_in, in_sem.at[0]), pltpu.make_async_copy(width_hbm, width_in, in_sem.at[1])]
    for copy in small:
        copy.start()
    barrier = pltpu.get_barrier_semaphore()
    for peer in row_peers + col_peers:
        pl.semaphore_signal(barrier, inc=1, device_id=peer, device_id_type=MESH)

    def near_chip(i):
        return ((x_hi + i // 4) % 2) * 4 + (y + far_fourth(3 - i % 4)) % 4

    def chip_rows(i):
        return pl.ds(pl.multiple_of(near_chip(i) * width, width), width)

    def load(i):
        at = chip_rows(i)
        return pltpu.make_async_copy(s_hbm.at[at], s_f32.at[at], s_sem.at[i])

    def start_load(i, _):
        load(i).start()
        return 0

    lax.fori_loop(0, chips, start_load, 0)

    for copy in small:
        copy.wait()
    lanes = lax.broadcasted_iota(jnp.int32, (4, PAD), 1)
    shift = odd * (PAD - modes)
    mine = (lanes >= shift) & (lanes < shift + modes)
    fresh = jnp.concatenate([b_in[...], width_in[...]], axis=0)
    fresh = jnp.concatenate([fresh, jnp.zeros((4, PAD - modes), F32)], axis=1)
    own_b = jnp.where(odd == 1, pltpu.roll(fresh, PAD - modes, 1), fresh)
    a_slot[col] = own_b
    pl.semaphore_wait(barrier, rows_n + cols_n - 2)

    def send(src, dst, peer, at, arrived=None):
        copy = pltpu.make_async_remote_copy(
            src_ref=src, dst_ref=dst, send_sem=send_sem.at[at],
            recv_sem=recv_sem.at[at] if arrived is None else arrived,
            device_id=peer, device_id_type=MESH)
        copy.start()

    for peer in row_peers:
        send(a_slot.at[col], a_slot.at[col], peer, 0, a_sem.at[col])

    def split(i):
        load(i).wait()

        def some(k, _):
            at = pl.ds(pl.multiple_of(near_chip(i) * width + k * 64, 64), 64)
            whole = s_f32[at]
            high = whole.astype(BF16)
            s_hi[at] = high
            s_lo[at] = (whole - high.astype(F32)).astype(BF16)
            return 0

        lax.fori_loop(0, width // 64, some, 0)

    early = chips // 2

    def prepare(i, _):
        split(i)
        return 0

    lax.fori_loop(0, early, prepare, 0)

    total = jnp.zeros((16, block_cols), F32)
    for i in range(chips):
        if i >= early:
            split(i)
        chip = near_chip(i)
        for j in range(2):
            @pl.when(2 * chip + j != col)
            def _():
                arrived = a_slot.at[2 * chip + j]
                pltpu.make_async_copy(arrived, arrived, a_sem.at[2 * chip + j]).wait()

        left, right = a_slot[2 * chip], a_slot[2 * chip + 1]
        vector = jnp.concatenate([left[:, :LANES], left[:, LANES:] + right[:, :LANES], right[:, LANES:]], axis=1)
        at = chip_rows(i)
        v_buf[:, at] = vector
        part = three_parts(vector)
        total = total + jnp.dot(part, s_hi[at], preferred_element_type=F32)
        total = total + jnp.dot(part, s_lo[at], preferred_element_type=F32)
    on_diagonal = row == col // 2
    half = v_buf[:, pl.ds(pl.multiple_of(odd * block_cols, LANES), block_cols)]
    flag = jnp.where(on_diagonal, 1.0, 0.0).astype(F32)
    p_slot[row] = joined(total) + half * half[3:4] * flag
    for peer in col_peers:
        send(p_slot.at[row], p_slot.at[row], peer, 1)

    turned = t_hi.shape[1]
    per_chip = width // LANES

    def turn(i, _):
        rows = pl.ds(pl.multiple_of(near_chip(i // per_chip) * width + (i % per_chip) * LANES, LANES), LANES)
        at = pl.ds(pl.multiple_of(i * LANES, LANES), LANES)
        t_hi[:, at] = s_hi[rows].T
        t_lo[:, at] = s_lo[rows].T
        return 0

    lax.fori_loop(0, turned // LANES, turn, 0)
    await_bytes(p_slot, rows_n - 1, recv_sem.at[1])
    w1 = p_slot[0]
    for i in range(1, rows_n):
        w1 = w1 + p_slot[i]
    w_buf[...] = w1

    home = col // 2
    y_to = (y + 2 - z + home // 2) % 4
    across = jnp.where(x_lo == home % 2, 0, 1)
    for core in range(2):
        send(w_buf, f_slot.at[odd], (home, ((x_hi + across) % 2) * 8 + y_to * 2 + core), 2)

    def window(j):
        return pl.ds(pl.multiple_of((j // 2) * width + (j % 2) * LANES, LANES), PAD)

    w_parts = three_parts(w1)
    near = jnp.dot(w_parts, t_hi[...], preferred_element_type=F32)
    near = joined(near + jnp.dot(w_parts, t_lo[...], preferred_element_type=F32))
    for i in range(chips):
        at = chip_rows(i)
        if (i + 1) * width <= turned:
            q_buf[:, at] = near[:, i * width:(i + 1) * width]
        else:
            dims = (((1,), (1,)), ((), ()))
            out = lax.dot_general(w_parts, s_hi[at], dims, preferred_element_type=F32)
            q_buf[:, at] = joined(out + lax.dot_general(w_parts, s_lo[at], dims, preferred_element_type=F32))
    d_slot[col] = q_buf[:, window(col)]

    await_bytes(f_slot, 2, recv_sem.at[2])
    per_block = block_cols // modes
    own_w1 = jnp.where(mine, f_slot[col // per_block, :, window(col % per_block)], 0.0)

    def inner(u, v):
        return jnp.sum(u * v, axis=1, keepdims=True)

    cross = jnp.zeros((4, LANES), F32)
    per_half = block_cols // LANES
    for i in range(block_rows // LANES):
        part = f_slot[i // per_half, :, (i % per_half) * LANES:(i % per_half + 1) * LANES]
        cross = cross + part * q_buf[:, i * LANES:(i + 1) * LANES]
    last = jnp.sum(cross, axis=1, keepdims=True) + inner(own_b[3:4] * own_w1, own_w1)
    lane = lax.broadcasted_iota(jnp.int32, (4, LANES), 1)
    table = jnp.zeros((4, LANES), F32)
    for i, moment in enumerate([inner(own_b, own_b), inner(own_b, own_w1), inner(own_w1, own_w1), last]):
        table = jnp.where(lane == i, moment, table)
    line = table[0:1] + pltpu.roll(table[1:2], 4, 1) + pltpu.roll(table[2:3], 8, 1)
    e_slot[pl.ds(me, 1)] = line

    def tell(peers):
        for peer in peers:
            send(e_slot.at[pl.ds(me, 1)], e_slot.at[pl.ds(me, 1)], peer, 4)

    tell(everyone[:FAR])
    for to_row, to_col in row_peers:
        send(q_buf.at[:, window(to_col)], d_slot.at[col], (to_row, to_col), 3)
    tell(everyone[FAR:])

    await_bytes(d_slot, cols_n - 1, recv_sem.at[3])
    w2 = d_slot[0]
    for i in range(1, cols_n):
        w2 = w2 + d_slot[i]
    own_w2 = jnp.where(mine, w2, 0.0) + own_b[3:4] * own_w1

    n = rows_n * cols_n
    await_bytes(e_slot, n - 1, recv_sem.at[4])
    line = jnp.sum(e_slot[...], axis=0, keepdims=True)
    g = jnp.concatenate([line, pltpu.roll(line, LANES - 4, 1), pltpu.roll(line, LANES - 8, 1), line], axis=0)
    g0, g1, g2, g3 = (g[:, i:i + 1] for i in range(4))
    a0 = g0 / g1
    norm = g0 - 2.0 * a0 * g1 + a0 * a0 * g2
    beta = norm / g0
    more = 1.0 + beta
    a1 = norm / (more * more * g1 - 2.0 * more * a0 * g2 + a0 * a0 * g3)
    r1 = own_b - a0 * own_w1
    results = [a0 * own_b + a1 * (r1 + beta * own_b) - r1, r1, a1 * (more * own_w1 - a0 * own_w2)]
    for ref, value in zip((x_part, res_part, res_step), results):
        value = jnp.where(odd == 1, pltpu.roll(value, modes, 1), value)
        ref[...] = value[0:3, :modes]

    await_bytes(a_slot, cols_n - 1, send_sem.at[0])
    await_bytes(p_slot, rows_n - 1, send_sem.at[1])
    await_bytes(d_slot, cols_n - 1, send_sem.at[3])
    await_bytes(e_slot, n - 1, send_sem.at[4])

    await_bytes(f_slot, 2, send_sem.at[2])


def solution(mesh):
    rows_n, cols_n = mesh.shape["row"], mesh.shape["col"]
    n = rows_n * cols_n

    def body(right_side, linewidth, scattering):
        block_rows, block_cols = scattering.shape
        vmem, anywhere = pl.BlockSpec(memory_space=pltpu.VMEM), pl.BlockSpec(memory_space=pl.ANY)
        line = linewidth.reshape(1, -1)
        x_part, res_part, res_step = pl.pallas_call(
            functools.partial(kernel, rows_n, cols_n),
            out_shape=(pltpu.VMEM(right_side.shape, F32),) * 3,
            in_specs=[anywhere] * 3,
            out_specs=(vmem,) * 3,
            scratch_shapes=[
                pltpu.VMEM((block_rows, block_cols), F32),
                pltpu.VMEM((block_rows, block_cols), BF16),
                pltpu.VMEM((block_rows, block_cols), BF16),
                pltpu.VMEM((block_cols, block_rows // 8 * TURNED), BF16),
                pltpu.VMEM((block_cols, block_rows // 8 * TURNED), BF16),
                pltpu.VMEM(right_side.shape, F32),
                pltpu.VMEM(line.shape, F32),
                pltpu.VMEM((cols_n, 4, PAD), F32),
                pltpu.VMEM((4, block_rows), F32),
                pltpu.VMEM((rows_n, 4, block_cols), F32),
                pltpu.VMEM((4, block_cols), F32),
                pltpu.VMEM((2, 4, block_cols), F32),
                pltpu.VMEM((4, block_rows), F32),
                pltpu.VMEM((cols_n, 4, PAD), F32),
                pltpu.VMEM((n, LANES), F32),
                pltpu.SemaphoreType.DMA((cols_n // 2,)),
                pltpu.SemaphoreType.DMA((2,)),
                pltpu.SemaphoreType.DMA((cols_n,)),
                pltpu.SemaphoreType.DMA((5,)),
                pltpu.SemaphoreType.DMA((5,)),
            ],
            compiler_params=pltpu.CompilerParams(
                collective_id=0, has_side_effects=True, vmem_limit_bytes=60 << 20),
        )(right_side, line, scattering)
        return x_part + res_part, res_part - res_step

    return jax.shard_map(
        body,
        mesh=mesh,
        in_specs=(P(None, ROW_COL), P(ROW_COL), P("row", "col")),
        out_specs=(P(None, ROW_COL), P(None, ROW_COL)),
        check_vma=False,
    )
```

```python
import functools

import jax
import jax.numpy as jnp
from jax import lax
from jax.experimental import pallas as pl
from jax.experimental.pallas import tpu as pltpu
from jax.sharding import PartitionSpec as P

ROW_COL = ("row", "col")
MESH = pl.DeviceIdType.MESH
F32, BF16 = jnp.float32, jnp.bfloat16
LANES = 128
TURNED = 5
FAR = 44
PAD = 2 * LANES


def three_parts(rows):
    top = rows.astype(BF16).astype(F32)
    rest = rows - top
    middle = rest.astype(BF16).astype(F32)
    low = rest - middle
    return jnp.concatenate([top, middle, low, jnp.zeros_like(low)], axis=0).astype(BF16)


def joined(product):
    return product[0:4] + product[4:8] + product[8:12]


def await_bytes(ref, count, sem):
    part = ref.at[pl.ds(0, count)]
    pltpu.make_async_copy(part, part, sem).wait()


def ring(d):
    return min(d, 4 - d)


def farthest_first(offsets):
    hops = lambda o: ring(o[0]) + ring(o[1]) + ring(o[2]) + 0.1 * o[3]
    return sorted((o for o in offsets if any(o)), key=lambda o: -hops(o))


def far_fourth(j):
    return 2 - j + 3 * (j // 2) - 2 * ((j + 1) // 4)


def kernel(rows_n, cols_n, b_hbm, width_hbm, s_hbm, x_part, res_part, res_step,
           s_f32, s_hi, s_lo, t_hi, t_lo, b_in, width_in, a_slot, v_buf, p_slot, w_buf, f_slot, q_buf,
           d_slot, e_slot, s_sem, in_sem, a_sem, send_sem, recv_sem):
    row, col = lax.axis_index("row"), lax.axis_index("col")
    me = row * cols_n + col
    block_rows, block_cols = s_f32.shape
    modes = b_in.shape[1]
    chips = cols_n // 2
    width = 2 * modes
    odd = lax.rem(col, 2)

    z, x_lo, x_hi, y = row // 2, lax.rem(row, 2), col // 8, lax.rem(col // 2, 4)
    x = x_hi * 2 + x_lo
    z_at = [lax.rem(z + d, 4) * 2 for d in range(4)]
    y_at = [lax.rem(y + d, 4) * 2 for d in range(4)]
    x_hi_at = [x_hi * 8, 8 - x_hi * 8]
    core_at = [odd, 1 - odd]

    row_peers = [(row, x_hi_at[dx // 2] + y_at[dy] + core_at[dc]) for _, dy, dx, dc in
                 farthest_first([(0, dy, dx, dc) for dy in range(4) for dx in (0, 2) for dc in (0, 1)])]
    col_peers = [(z_at[dz] + (1 - x_lo if dx else x_lo), col) for dz, _, dx, _ in
                 farthest_first([(dz, 0, dx, 0) for dz in range(4) for dx in (0, 1)])]
    barrier = pltpu.get_barrier_semaphore()
    for peer in row_peers + col_peers:
        pl.semaphore_signal(barrier, inc=1, device_id=peer, device_id_type=MESH)
    small = [pltpu.make_async_copy(b_hbm, b_in, in_sem.at[0]), pltpu.make_async_copy(width_hbm, width_in, in_sem.at[1])]
    for copy in small:
        copy.start()

    def near_chip(i):
        return ((x_hi + i // 4) % 2) * 4 + (y + far_fourth(3 - i % 4)) % 4

    def chip_rows(i):
        return pl.ds(pl.multiple_of(near_chip(i) * width, width), width)

    def load(i):
        at = chip_rows(i)
        return pltpu.make_async_copy(s_hbm.at[at], s_f32.at[at], s_sem.at[i])

    def start_load(i, _):
        load(i).start()
        return 0

    lax.fori_loop(0, chips, start_load, 0)

    for copy in small:
        copy.wait()
    lanes = lax.broadcasted_iota(jnp.int32, (4, PAD), 1)
    shift = odd * (PAD - modes)
    mine = (lanes >= shift) & (lanes < shift + modes)
    fresh = jnp.concatenate([b_in[...], width_in[...]], axis=0)
    fresh = jnp.concatenate([fresh, jnp.zeros((4, PAD - modes), F32)], axis=1)
    own_b = jnp.where(odd == 1, pltpu.roll(fresh, PAD - modes, 1), fresh)
    a_slot[col] = own_b
    pl.semaphore_wait(barrier, rows_n + cols_n - 2)

    def send(src, dst, peer, at, arrived=None):
        copy = pltpu.make_async_remote_copy(
            src_ref=src, dst_ref=dst, send_sem=send_sem.at[at],
            recv_sem=recv_sem.at[at] if arrived is None else arrived,
            device_id=peer, device_id_type=MESH)
        copy.start()

    for peer in row_peers:
        send(a_slot.at[col], a_slot.at[col], peer, 0, a_sem.at[col])

    def split(i):
        load(i).wait()

        def some(k, _):
            at = pl.ds(pl.multiple_of(near_chip(i) * width + k * 192, 192), 192)
            whole = s_f32[at]
            high = whole.astype(BF16)
            s_hi[at] = high
            s_lo[at] = (whole - high.astype(F32)).astype(BF16)
            return 0

        lax.fori_loop(0, width // 192, some, 0)

    early = chips - 1

    def prepare(i, _):
        split(i)
        return 0

    lax.fori_loop(0, early, prepare, 0)

    total = jnp.zeros((16, block_cols), F32)
    for i in range(chips):
        if i >= early:
            split(i)
        chip = near_chip(i)
        for j in range(2):
            @pl.when(2 * chip + j != col)
            def _():
                arrived = a_slot.at[2 * chip + j]
                pltpu.make_async_copy(arrived, arrived, a_sem.at[2 * chip + j]).wait()

        left, right = a_slot[2 * chip], a_slot[2 * chip + 1]
        vector = jnp.concatenate([left[:, :LANES], left[:, LANES:] + right[:, :LANES], right[:, LANES:]], axis=1)
        at = chip_rows(i)
        v_buf[:, at] = vector
        part = three_parts(vector)
        total = total + jnp.dot(part, s_hi[at], preferred_element_type=F32)
        total = total + jnp.dot(part, s_lo[at], preferred_element_type=F32)
    on_diagonal = row == col // 2
    half = v_buf[:, pl.ds(pl.multiple_of(odd * block_cols, LANES), block_cols)]
    flag = jnp.where(on_diagonal, 1.0, 0.0).astype(F32)
    p_slot[row] = joined(total) + half * half[3:4] * flag
    for peer in col_peers:
        send(p_slot.at[row], p_slot.at[row], peer, 1)

    turned = t_hi.shape[1]
    per_chip = width // LANES

    def turn(i, _):
        rows = pl.ds(pl.multiple_of(near_chip(i // per_chip) * width + (i % per_chip) * LANES, LANES), LANES)
        at = pl.ds(pl.multiple_of(i * LANES, LANES), LANES)
        t_hi[:, at] = s_hi[rows].T
        t_lo[:, at] = s_lo[rows].T
        return 0

    lax.fori_loop(0, turned // LANES, turn, 0)
    await_bytes(p_slot, rows_n - 1, recv_sem.at[1])
    w1 = p_slot[0]
    for i in range(1, rows_n):
        w1 = w1 + p_slot[i]
    w_buf[...] = w1

    home = col // 2
    y_to = (y + 2 - z + home // 2) % 4
    across = jnp.where(x_lo == home % 2, 0, 1)
    for core in range(2):
        send(w_buf, f_slot.at[odd], (home, ((x_hi + across) % 2) * 8 + y_to * 2 + core), 2)

    def window(j):
        return pl.ds(pl.multiple_of((j // 2) * width + (j % 2) * LANES, LANES), PAD)

    w_parts = three_parts(w1)
    near = jnp.dot(w_parts, t_hi[...], preferred_element_type=F32)
    near = joined(near + jnp.dot(w_parts, t_lo[...], preferred_element_type=F32))
    for i in range(chips):
        at = chip_rows(i)
        if (i + 1) * width <= turned:
            q_buf[:, at] = near[:, i * width:(i + 1) * width]
        else:
            dims = (((1,), (1,)), ((), ()))
            out = lax.dot_general(w_parts, s_hi[at], dims, preferred_element_type=F32)
            q_buf[:, at] = joined(out + lax.dot_general(w_parts, s_lo[at], dims, preferred_element_type=F32))
    d_slot[col] = q_buf[:, window(col)]

    await_bytes(f_slot, 2, recv_sem.at[2])
    per_block = block_cols // modes
    own_w1 = jnp.where(mine, f_slot[col // per_block, :, window(col % per_block)], 0.0)

    def inner(u, v):
        return jnp.sum(u * v, axis=1, keepdims=True)

    cross = jnp.zeros((4, LANES), F32)
    per_half = block_cols // LANES
    for i in range(block_rows // LANES):
        part = f_slot[i // per_half, :, (i % per_half) * LANES:(i % per_half + 1) * LANES]
        cross = cross + part * q_buf[:, i * LANES:(i + 1) * LANES]
    last = jnp.sum(cross, axis=1, keepdims=True) + inner(own_b[3:4] * own_w1, own_w1)
    lane = lax.broadcasted_iota(jnp.int32, (4, LANES), 1)
    table = jnp.zeros((4, LANES), F32)
    for i, moment in enumerate([inner(own_b, own_b), inner(own_b, own_w1), inner(own_w1, own_w1), last]):
        table = jnp.where(lane == i, moment, table)
    line = table[0:1] + pltpu.roll(table[1:2], 4, 1) + pltpu.roll(table[2:3], 8, 1)
    e_slot[pl.ds(me, 1)] = line

    x_at = [lax.rem(x + d, 4) for d in range(4)]
    x_row = [lax.rem(at, 2) for at in x_at]
    x_col = [at // 2 * 8 for at in x_at]
    everyone = [(z_at[dz] + x_row[dx], x_col[dx] + y_at[dy] + core_at[dc]) for dz, dy, dx, dc in farthest_first(
        [(dz, dy, dx, dc) for dz in range(4) for dy in range(4) for dx in range(4) for dc in (0, 1)])]

    def tell(peers):
        for peer in peers:
            send(e_slot.at[pl.ds(me, 1)], e_slot.at[pl.ds(me, 1)], peer, 4)

    tell(everyone[:FAR])
    for to_row, to_col in row_peers:
        send(q_buf.at[:, window(to_col)], d_slot.at[col], (to_row, to_col), 3)
    tell(everyone[FAR:])

    await_bytes(d_slot, cols_n - 1, recv_sem.at[3])
    w2 = d_slot[0]
    for i in range(1, cols_n):
        w2 = w2 + d_slot[i]
    own_w2 = jnp.where(mine, w2, 0.0) + own_b[3:4] * own_w1
    own_b, own_w1, own_w2 = (
        jnp.where(odd == 1, pltpu.roll(value, modes, 1), value)[:, :modes] for value in (own_b, own_w1, own_w2))

    n = rows_n * cols_n
    await_bytes(e_slot, n - 1, recv_sem.at[4])
    line = jnp.sum(e_slot[...], axis=0, keepdims=True)
    g = jnp.concatenate([line, pltpu.roll(line, LANES - 4, 1), pltpu.roll(line, LANES - 8, 1), line], axis=0)
    g0, g1, g2, g3 = (g[:, i:i + 1] for i in range(4))
    a0 = g0 / g1
    norm = g0 - 2.0 * a0 * g1 + a0 * a0 * g2
    beta = norm / g0
    more = 1.0 + beta
    a1 = norm / (more * more * g1 - 2.0 * more * a0 * g2 + a0 * a0 * g3)
    r1 = own_b - a0 * own_w1
    results = [a0 * own_b + a1 * (r1 + beta * own_b) - r1, r1, a1 * (more * own_w1 - a0 * own_w2)]
    for ref, value in zip((x_part, res_part, res_step), results):
        ref[...] = value[0:3]

    await_bytes(a_slot, cols_n - 1, send_sem.at[0])
    await_bytes(p_slot, rows_n - 1, send_sem.at[1])
    await_bytes(d_slot, cols_n - 1, send_sem.at[3])
    await_bytes(e_slot, n - 1, send_sem.at[4])

    await_bytes(f_slot, 2, send_sem.at[2])


def solution(mesh):
    rows_n, cols_n = mesh.shape["row"], mesh.shape["col"]
    n = rows_n * cols_n

    def body(right_side, linewidth, scattering):
        block_rows, block_cols = scattering.shape
        vmem, anywhere = pl.BlockSpec(memory_space=pltpu.VMEM), pl.BlockSpec(memory_space=pl.ANY)
        line = linewidth.reshape(1, -1)
        x_part, res_part, res_step = pl.pallas_call(
            functools.partial(kernel, rows_n, cols_n),
            out_shape=(pltpu.VMEM(right_side.shape, F32),) * 3,
            in_specs=[anywhere] * 3,
            out_specs=(vmem,) * 3,
            scratch_shapes=[
                pltpu.VMEM((block_rows, block_cols), F32),
                pltpu.VMEM((block_rows, block_cols), BF16),
                pltpu.VMEM((block_rows, block_cols), BF16),
                pltpu.VMEM((block_cols, block_rows // 8 * TURNED), BF16),
                pltpu.VMEM((block_cols, block_rows // 8 * TURNED), BF16),
                pltpu.VMEM(right_side.shape, F32),
                pltpu.VMEM(line.shape, F32),
                pltpu.VMEM((cols_n, 4, PAD), F32),
                pltpu.VMEM((4, block_rows), F32),
                pltpu.VMEM((rows_n, 4, block_cols), F32),
                pltpu.VMEM((4, block_cols), F32),
                pltpu.VMEM((2, 4, block_cols), F32),
                pltpu.VMEM((4, block_rows), F32),
                pltpu.VMEM((cols_n, 4, PAD), F32),
                pltpu.VMEM((n, LANES), F32),
                pltpu.SemaphoreType.DMA((cols_n // 2,)),
                pltpu.SemaphoreType.DMA((2,)),
                pltpu.SemaphoreType.DMA((cols_n,)),
                pltpu.SemaphoreType.DMA((5,)),
                pltpu.SemaphoreType.DMA((5,)),
            ],
            compiler_params=pltpu.CompilerParams(
                collective_id=0, has_side_effects=True, vmem_limit_bytes=60 << 20),
        )(right_side, line, scattering)
        return x_part + res_part, res_part - res_step

    return jax.shard_map(
        body,
        mesh=mesh,
        in_specs=(P(None, ROW_COL), P(ROW_COL), P("row", "col")),
        out_specs=(P(None, ROW_COL), P(None, ROW_COL)),
        check_vma=False,
    )
```

```python
import functools

import jax
import jax.numpy as jnp
from jax import lax
from jax.experimental import pallas as pl
from jax.experimental.pallas import tpu as pltpu
from jax.sharding import PartitionSpec as P

ROW_COL = ("row", "col")
MESH = pl.DeviceIdType.MESH
F32, BF16 = jnp.float32, jnp.bfloat16
LANES = 128
SPLIT_BEFORE = {1: (5,), 3: (6,), 5: (7,)}
TURNED = 5
FAR = 44
PAD = 2 * LANES


def three_parts(rows):
    top = rows.astype(BF16).astype(F32)
    rest = rows - top
    middle = rest.astype(BF16).astype(F32)
    low = rest - middle
    return jnp.concatenate([top, middle, low, jnp.zeros_like(low)], axis=0).astype(BF16)


def joined(product):
    return product[0:4] + product[4:8] + product[8:12]


def await_bytes(ref, count, sem):
    part = ref.at[pl.ds(0, count)]
    pltpu.make_async_copy(part, part, sem).wait()


def ring(d):
    return min(d, 4 - d)


def farthest_first(offsets):
    hops = lambda o: ring(o[0]) + ring(o[1]) + ring(o[2]) + 0.1 * o[3]
    return sorted((o for o in offsets if any(o)), key=lambda o: -hops(o))


def far_fourth(j):
    return 2 - j + 3 * (j // 2) - 2 * ((j + 1) // 4)


def kernel(rows_n, cols_n, b_hbm, width_hbm, s_hbm, x_part, res_part, res_step,
           s_f32, s_hi, s_lo, t_hi, t_lo, b_in, width_in, a_slot, v_buf, p_slot, w_buf, f_slot, q_buf,
           d_slot, e_slot, s_sem, in_sem, a_sem, send_sem, recv_sem):
    row, col = lax.axis_index("row"), lax.axis_index("col")
    me = row * cols_n + col
    block_rows, block_cols = s_f32.shape
    modes = b_in.shape[1]
    chips = cols_n // 2
    width = 2 * modes
    odd = lax.rem(col, 2)

    z, x_lo, x_hi, y = row // 2, lax.rem(row, 2), col // 8, lax.rem(col // 2, 4)
    x = x_hi * 2 + x_lo
    z_at = [lax.rem(z + d, 4) * 2 for d in range(4)]
    y_at = [lax.rem(y + d, 4) * 2 for d in range(4)]
    x_hi_at = [x_hi * 8, 8 - x_hi * 8]
    core_at = [odd, 1 - odd]

    row_peers = [(row, x_hi_at[dx // 2] + y_at[dy] + core_at[dc]) for _, dy, dx, dc in
                 farthest_first([(0, dy, dx, dc) for dy in range(4) for dx in (0, 2) for dc in (0, 1)])]
    col_peers = [(z_at[dz] + (1 - x_lo if dx else x_lo), col) for dz, _, dx, _ in
                 farthest_first([(dz, 0, dx, 0) for dz in range(4) for dx in (0, 1)])]
    barrier = pltpu.get_barrier_semaphore()
    for peer in row_peers + col_peers:
        pl.semaphore_signal(barrier, inc=1, device_id=peer, device_id_type=MESH)
    small = [pltpu.make_async_copy(b_hbm, b_in, in_sem.at[0]), pltpu.make_async_copy(width_hbm, width_in, in_sem.at[1])]
    for copy in small:
        copy.start()

    def near_chip(i):
        return ((x_hi + i // 4) % 2) * 4 + (y + far_fourth(3 - i % 4)) % 4

    def chip_rows(i):
        return pl.ds(pl.multiple_of(near_chip(i) * width, width), width)

    def load(i):
        at = chip_rows(i)
        return pltpu.make_async_copy(s_hbm.at[at], s_f32.at[at], s_sem.at[i])

    def start_load(i, _):
        load(i).start()
        return 0

    lax.fori_loop(0, chips, start_load, 0)

    for copy in small:
        copy.wait()
    lanes = lax.broadcasted_iota(jnp.int32, (4, PAD), 1)
    shift = odd * (PAD - modes)
    mine = (lanes >= shift) & (lanes < shift + modes)
    fresh = jnp.concatenate([b_in[...], width_in[...]], axis=0)
    fresh = jnp.concatenate([fresh, jnp.zeros((4, PAD - modes), F32)], axis=1)
    own_b = jnp.where(odd == 1, pltpu.roll(fresh, PAD - modes, 1), fresh)
    a_slot[col] = own_b
    pl.semaphore_wait(barrier, rows_n + cols_n - 2)

    def send(src, dst, peer, at, arrived=None):
        copy = pltpu.make_async_remote_copy(
            src_ref=src, dst_ref=dst, send_sem=send_sem.at[at],
            recv_sem=recv_sem.at[at] if arrived is None else arrived,
            device_id=peer, device_id_type=MESH)
        copy.start()

    for peer in row_peers:
        send(a_slot.at[col], a_slot.at[col], peer, 0, a_sem.at[col])

    def split(i):
        load(i).wait()

        def some(k, _):
            at = pl.ds(pl.multiple_of(near_chip(i) * width + k * 192, 192), 192)
            whole = s_f32[at]
            high = whole.astype(BF16)
            s_hi[at] = high
            s_lo[at] = (whole - high.astype(F32)).astype(BF16)
            return 0

        lax.fori_loop(0, width // 192, some, 0)

    early = chips - 3

    def prepare(i, _):
        split(i)
        return 0

    lax.fori_loop(0, early, prepare, 0)

    total = jnp.zeros((16, block_cols), F32)
    for i in range(chips):
        for late in SPLIT_BEFORE.get(i, ()):
            split(late)
        chip = near_chip(i)
        for j in range(2):
            @pl.when(2 * chip + j != col)
            def _():
                arrived = a_slot.at[2 * chip + j]
                pltpu.make_async_copy(arrived, arrived, a_sem.at[2 * chip + j]).wait()

        left, right = a_slot[2 * chip], a_slot[2 * chip + 1]
        vector = jnp.concatenate([left[:, :LANES], left[:, LANES:] + right[:, :LANES], right[:, LANES:]], axis=1)
        at = chip_rows(i)
        v_buf[:, at] = vector
        part = three_parts(vector)
        total = total + jnp.dot(part, s_hi[at], preferred_element_type=F32)
        total = total + jnp.dot(part, s_lo[at], preferred_element_type=F32)
    on_diagonal = row == col // 2
    half = v_buf[:, pl.ds(pl.multiple_of(odd * block_cols, LANES), block_cols)]
    flag = jnp.where(on_diagonal, 1.0, 0.0).astype(F32)
    p_slot[row] = joined(total) + half * half[3:4] * flag
    for peer in col_peers:
        send(p_slot.at[row], p_slot.at[row], peer, 1)

    turned = t_hi.shape[1]
    per_chip = width // LANES

    def turn(i, _):
        rows = pl.ds(pl.multiple_of(near_chip(i // per_chip) * width + (i % per_chip) * LANES, LANES), LANES)
        at = pl.ds(pl.multiple_of(i * LANES, LANES), LANES)
        t_hi[:, at] = s_hi[rows].T
        t_lo[:, at] = s_lo[rows].T
        return 0

    lax.fori_loop(0, turned // LANES, turn, 0)
    await_bytes(p_slot, rows_n - 1, recv_sem.at[1])
    w1 = p_slot[0]
    for i in range(1, rows_n):
        w1 = w1 + p_slot[i]
    w_buf[...] = w1

    home = col // 2
    y_to = (y + 2 - z + home // 2) % 4
    across = jnp.where(x_lo == home % 2, 0, 1)
    for core in range(2):
        send(w_buf, f_slot.at[odd], (home, ((x_hi + across) % 2) * 8 + y_to * 2 + core), 2)

    def window(j):
        return pl.ds(pl.multiple_of((j // 2) * width + (j % 2) * LANES, LANES), PAD)

    w_parts = three_parts(w1)
    near = jnp.dot(w_parts, t_hi[...], preferred_element_type=F32)
    near = joined(near + jnp.dot(w_parts, t_lo[...], preferred_element_type=F32))
    for i in range(chips):
        at = chip_rows(i)
        if (i + 1) * width <= turned:
            q_buf[:, at] = near[:, i * width:(i + 1) * width]
        else:
            dims = (((1,), (1,)), ((), ()))
            out = lax.dot_general(w_parts, s_hi[at], dims, preferred_element_type=F32)
            q_buf[:, at] = joined(out + lax.dot_general(w_parts, s_lo[at], dims, preferred_element_type=F32))
    d_slot[col] = q_buf[:, window(col)]

    await_bytes(f_slot, 2, recv_sem.at[2])
    per_block = block_cols // modes
    own_w1 = jnp.where(mine, f_slot[col // per_block, :, window(col % per_block)], 0.0)

    def inner(u, v):
        return jnp.sum(u * v, axis=1, keepdims=True)

    cross = jnp.zeros((4, LANES), F32)
    per_half = block_cols // LANES
    for i in range(block_rows // LANES):
        part = f_slot[i // per_half, :, (i % per_half) * LANES:(i % per_half + 1) * LANES]
        cross = cross + part * q_buf[:, i * LANES:(i + 1) * LANES]
    last = jnp.sum(cross, axis=1, keepdims=True) + inner(own_b[3:4] * own_w1, own_w1)
    lane = lax.broadcasted_iota(jnp.int32, (4, LANES), 1)
    table = jnp.zeros((4, LANES), F32)
    for i, moment in enumerate([inner(own_b, own_b), inner(own_b, own_w1), inner(own_w1, own_w1), last]):
        table = jnp.where(lane == i, moment, table)
    line = table[0:1] + pltpu.roll(table[1:2], 4, 1) + pltpu.roll(table[2:3], 8, 1)
    e_slot[pl.ds(me, 1)] = line

    x_at = [lax.rem(x + d, 4) for d in range(4)]
    x_row = [lax.rem(at, 2) for at in x_at]
    x_col = [at // 2 * 8 for at in x_at]
    everyone = [(z_at[dz] + x_row[dx], x_col[dx] + y_at[dy] + core_at[dc]) for dz, dy, dx, dc in farthest_first(
        [(dz, dy, dx, dc) for dz in range(4) for dy in range(4) for dx in range(4) for dc in (0, 1)])]

    def tell(peers):
        for peer in peers:
            send(e_slot.at[pl.ds(me, 1)], e_slot.at[pl.ds(me, 1)], peer, 4)

    tell(everyone[:FAR])
    for to_row, to_col in row_peers:
        send(q_buf.at[:, window(to_col)], d_slot.at[col], (to_row, to_col), 3)
    tell(everyone[FAR:])

    await_bytes(d_slot, cols_n - 1, recv_sem.at[3])
    w2 = d_slot[0]
    for i in range(1, cols_n):
        w2 = w2 + d_slot[i]
    own_w2 = jnp.where(mine, w2, 0.0) + own_b[3:4] * own_w1
    own_b, own_w1, own_w2 = (
        jnp.where(odd == 1, pltpu.roll(value, modes, 1), value)[:, :modes] for value in (own_b, own_w1, own_w2))

    n = rows_n * cols_n
    await_bytes(e_slot, n - 1, recv_sem.at[4])
    line = jnp.sum(e_slot[...], axis=0, keepdims=True)
    g = jnp.concatenate([line, pltpu.roll(line, LANES - 4, 1), pltpu.roll(line, LANES - 8, 1), line], axis=0)
    g0, g1, g2, g3 = (g[:, i:i + 1] for i in range(4))
    a0 = g0 / g1
    norm = g0 - 2.0 * a0 * g1 + a0 * a0 * g2
    beta = norm / g0
    more = 1.0 + beta
    a1 = norm / (more * more * g1 - 2.0 * more * a0 * g2 + a0 * a0 * g3)
    r1 = own_b - a0 * own_w1
    results = [a0 * own_b + a1 * (r1 + beta * own_b) - r1, r1, a1 * (more * own_w1 - a0 * own_w2)]
    for ref, value in zip((x_part, res_part, res_step), results):
        ref[...] = value[0:3]

    await_bytes(a_slot, cols_n - 1, send_sem.at[0])
    await_bytes(p_slot, rows_n - 1, send_sem.at[1])
    await_bytes(d_slot, cols_n - 1, send_sem.at[3])
    await_bytes(e_slot, n - 1, send_sem.at[4])

    await_bytes(f_slot, 2, send_sem.at[2])


def solution(mesh):
    rows_n, cols_n = mesh.shape["row"], mesh.shape["col"]
    n = rows_n * cols_n

    def body(right_side, linewidth, scattering):
        block_rows, block_cols = scattering.shape
        vmem, anywhere = pl.BlockSpec(memory_space=pltpu.VMEM), pl.BlockSpec(memory_space=pl.ANY)
        line = linewidth.reshape(1, -1)
        x_part, res_part, res_step = pl.pallas_call(
            functools.partial(kernel, rows_n, cols_n),
            out_shape=(pltpu.VMEM(right_side.shape, F32),) * 3,
            in_specs=[anywhere] * 3,
            out_specs=(vmem,) * 3,
            scratch_shapes=[
                pltpu.VMEM((block_rows, block_cols), F32),
                pltpu.VMEM((block_rows, block_cols), BF16),
                pltpu.VMEM((block_rows, block_cols), BF16),
                pltpu.VMEM((block_cols, block_rows // 8 * TURNED), BF16),
                pltpu.VMEM((block_cols, block_rows // 8 * TURNED), BF16),
                pltpu.VMEM(right_side.shape, F32),
                pltpu.VMEM(line.shape, F32),
                pltpu.VMEM((cols_n, 4, PAD), F32),
                pltpu.VMEM((4, block_rows), F32),
                pltpu.VMEM((rows_n, 4, block_cols), F32),
                pltpu.VMEM((4, block_cols), F32),
                pltpu.VMEM((2, 4, block_cols), F32),
                pltpu.VMEM((4, block_rows), F32),
                pltpu.VMEM((cols_n, 4, PAD), F32),
                pltpu.VMEM((n, LANES), F32),
                pltpu.SemaphoreType.DMA((cols_n // 2,)),
                pltpu.SemaphoreType.DMA((2,)),
                pltpu.SemaphoreType.DMA((cols_n,)),
                pltpu.SemaphoreType.DMA((5,)),
                pltpu.SemaphoreType.DMA((5,)),
            ],
            compiler_params=pltpu.CompilerParams(
                collective_id=0, has_side_effects=True, vmem_limit_bytes=60 << 20),
        )(right_side, line, scattering)
        return x_part + res_part, res_part - res_step

    return jax.shard_map(
        body,
        mesh=mesh,
        in_specs=(P(None, ROW_COL), P(ROW_COL), P("row", "col")),
        out_specs=(P(None, ROW_COL), P(None, ROW_COL)),
        check_vma=False,
    )
```

```python
import functools

import jax
import jax.numpy as jnp
from jax import lax
from jax.experimental import pallas as pl
from jax.experimental.pallas import tpu as pltpu
from jax.sharding import PartitionSpec as P

ROW_COL = ("row", "col")
MESH = pl.DeviceIdType.MESH
F32, BF16 = jnp.float32, jnp.bfloat16
LANES = 128
SPLIT_BEFORE = {1: (4,), 2: (5,), 3: (6,), 5: (7,)}
TURNED = 5
FAR = 44
PAD = 2 * LANES


def three_parts(rows):
    top = rows.astype(BF16).astype(F32)
    rest = rows - top
    middle = rest.astype(BF16).astype(F32)
    low = rest - middle
    return jnp.concatenate([top, middle, low, jnp.zeros_like(low)], axis=0).astype(BF16)


def joined(product):
    return product[0:4] + product[4:8] + product[8:12]


def await_bytes(ref, count, sem):
    part = ref.at[pl.ds(0, count)]
    pltpu.make_async_copy(part, part, sem).wait()


def ring(d):
    return min(d, 4 - d)


def farthest_first(offsets):
    hops = lambda o: ring(o[0]) + ring(o[1]) + ring(o[2]) + 0.1 * o[3]
    return sorted((o for o in offsets if any(o)), key=lambda o: -hops(o))


def far_fourth(j):
    return 2 - j + 3 * (j // 2) - 2 * ((j + 1) // 4)


def kernel(rows_n, cols_n, b_hbm, width_hbm, s_hbm, x_part, res_part, res_step,
           s_f32, s_hi, s_lo, t_hi, t_lo, b_in, width_in, a_slot, v_buf, p_slot, w_buf, f_slot, q_buf,
           d_slot, e_slot, s_sem, in_sem, a_sem, send_sem, recv_sem):
    row, col = lax.axis_index("row"), lax.axis_index("col")
    me = row * cols_n + col
    block_rows, block_cols = s_f32.shape
    modes = b_in.shape[1]
    chips = cols_n // 2
    width = 2 * modes
    odd = lax.rem(col, 2)

    z, x_lo, x_hi, y = row // 2, lax.rem(row, 2), col // 8, lax.rem(col // 2, 4)
    x = x_hi * 2 + x_lo
    z_at = [lax.rem(z + d, 4) * 2 for d in range(4)]
    y_at = [lax.rem(y + d, 4) * 2 for d in range(4)]
    x_hi_at = [x_hi * 8, 8 - x_hi * 8]
    core_at = [odd, 1 - odd]

    row_peers = [(row, x_hi_at[dx // 2] + y_at[dy] + core_at[dc]) for _, dy, dx, dc in
                 farthest_first([(0, dy, dx, dc) for dy in range(4) for dx in (0, 2) for dc in (0, 1)])]
    col_peers = [(z_at[dz] + (1 - x_lo if dx else x_lo), col) for dz, _, dx, _ in
                 farthest_first([(dz, 0, dx, 0) for dz in range(4) for dx in (0, 1)])]
    barrier = pltpu.get_barrier_semaphore()
    for peer in row_peers + col_peers:
        pl.semaphore_signal(barrier, inc=1, device_id=peer, device_id_type=MESH)
    small = [pltpu.make_async_copy(b_hbm, b_in, in_sem.at[0]), pltpu.make_async_copy(width_hbm, width_in, in_sem.at[1])]
    for copy in small:
        copy.start()

    def near_chip(i):
        return ((x_hi + i // 4) % 2) * 4 + (y + far_fourth(3 - i % 4)) % 4

    def chip_rows(i):
        return pl.ds(pl.multiple_of(near_chip(i) * width, width), width)

    def load(i):
        at = chip_rows(i)
        return pltpu.make_async_copy(s_hbm.at[at], s_f32.at[at], s_sem.at[i])

    def start_load(i, _):
        load(i).start()
        return 0

    lax.fori_loop(0, chips, start_load, 0)

    for copy in small:
        copy.wait()
    lanes = lax.broadcasted_iota(jnp.int32, (4, PAD), 1)
    shift = odd * (PAD - modes)
    mine = (lanes >= shift) & (lanes < shift + modes)
    fresh = jnp.concatenate([b_in[...], width_in[...]], axis=0)
    fresh = jnp.concatenate([fresh, jnp.zeros((4, PAD - modes), F32)], axis=1)
    own_b = jnp.where(odd == 1, pltpu.roll(fresh, PAD - modes, 1), fresh)
    a_slot[col] = own_b
    pl.semaphore_wait(barrier, rows_n + cols_n - 2)

    def send(src, dst, peer, at, arrived=None):
        copy = pltpu.make_async_remote_copy(
            src_ref=src, dst_ref=dst, send_sem=send_sem.at[at],
            recv_sem=recv_sem.at[at] if arrived is None else arrived,
            device_id=peer, device_id_type=MESH)
        copy.start()

    for peer in row_peers:
        send(a_slot.at[col], a_slot.at[col], peer, 0, a_sem.at[col])

    def split(i):
        load(i).wait()

        def some(k, _):
            at = pl.ds(pl.multiple_of(near_chip(i) * width + k * 192, 192), 192)
            whole = s_f32[at]
            high = whole.astype(BF16)
            s_hi[at] = high
            s_lo[at] = (whole - high.astype(F32)).astype(BF16)
            return 0

        lax.fori_loop(0, width // 192, some, 0)

    early = chips - 4

    def prepare(i, _):
        split(i)
        return 0

    lax.fori_loop(0, early, prepare, 0)

    total = jnp.zeros((16, block_cols), F32)
    for i in range(chips):
        for late in SPLIT_BEFORE.get(i, ()):
            split(late)
        chip = near_chip(i)
        for j in range(2):
            @pl.when(2 * chip + j != col)
            def _():
                arrived = a_slot.at[2 * chip + j]
                pltpu.make_async_copy(arrived, arrived, a_sem.at[2 * chip + j]).wait()

        left, right = a_slot[2 * chip], a_slot[2 * chip + 1]
        vector = jnp.concatenate([left[:, :LANES], left[:, LANES:] + right[:, :LANES], right[:, LANES:]], axis=1)
        at = chip_rows(i)
        v_buf[:, at] = vector
        part = three_parts(vector)
        total = total + jnp.dot(part, s_hi[at], preferred_element_type=F32)
        total = total + jnp.dot(part, s_lo[at], preferred_element_type=F32)
    on_diagonal = row == col // 2
    half = v_buf[:, pl.ds(pl.multiple_of(odd * block_cols, LANES), block_cols)]
    flag = jnp.where(on_diagonal, 1.0, 0.0).astype(F32)
    p_slot[row] = joined(total) + half * half[3:4] * flag
    for peer in col_peers:
        send(p_slot.at[row], p_slot.at[row], peer, 1)

    turned = t_hi.shape[1]
    per_chip = width // LANES

    def turn(i, _):
        rows = pl.ds(pl.multiple_of(near_chip(i // per_chip) * width + (i % per_chip) * LANES, LANES), LANES)
        at = pl.ds(pl.multiple_of(i * LANES, LANES), LANES)
        t_hi[:, at] = s_hi[rows].T
        t_lo[:, at] = s_lo[rows].T
        return 0

    lax.fori_loop(0, turned // LANES, turn, 0)
    await_bytes(p_slot, rows_n - 1, recv_sem.at[1])
    w1 = p_slot[0]
    for i in range(1, rows_n):
        w1 = w1 + p_slot[i]
    w_buf[...] = w1

    home = col // 2
    y_to = (y + 2 - z + home // 2) % 4
    across = jnp.where(x_lo == home % 2, 0, 1)
    for core in range(2):
        send(w_buf, f_slot.at[odd], (home, ((x_hi + across) % 2) * 8 + y_to * 2 + core), 2)

    def window(j):
        return pl.ds(pl.multiple_of((j // 2) * width + (j % 2) * LANES, LANES), PAD)

    w_parts = three_parts(w1)
    near = jnp.dot(w_parts, t_hi[...], preferred_element_type=F32)
    near = joined(near + jnp.dot(w_parts, t_lo[...], preferred_element_type=F32))
    for i in range(chips):
        at = chip_rows(i)
        if (i + 1) * width <= turned:
            q_buf[:, at] = near[:, i * width:(i + 1) * width]
        else:
            dims = (((1,), (1,)), ((), ()))
            out = lax.dot_general(w_parts, s_hi[at], dims, preferred_element_type=F32)
            q_buf[:, at] = joined(out + lax.dot_general(w_parts, s_lo[at], dims, preferred_element_type=F32))
    d_slot[col] = q_buf[:, window(col)]

    await_bytes(f_slot, 2, recv_sem.at[2])
    per_block = block_cols // modes
    own_w1 = jnp.where(mine, f_slot[col // per_block, :, window(col % per_block)], 0.0)

    def inner(u, v):
        return jnp.sum(u * v, axis=1, keepdims=True)

    cross = jnp.zeros((4, LANES), F32)
    per_half = block_cols // LANES
    for i in range(block_rows // LANES):
        part = f_slot[i // per_half, :, (i % per_half) * LANES:(i % per_half + 1) * LANES]
        cross = cross + part * q_buf[:, i * LANES:(i + 1) * LANES]
    last = jnp.sum(cross, axis=1, keepdims=True) + inner(own_b[3:4] * own_w1, own_w1)
    lane = lax.broadcasted_iota(jnp.int32, (4, LANES), 1)
    table = jnp.zeros((4, LANES), F32)
    for i, moment in enumerate([inner(own_b, own_b), inner(own_b, own_w1), inner(own_w1, own_w1), last]):
        table = jnp.where(lane == i, moment, table)
    line = table[0:1] + pltpu.roll(table[1:2], 4, 1) + pltpu.roll(table[2:3], 8, 1)
    e_slot[pl.ds(me, 1)] = line

    x_at = [lax.rem(x + d, 4) for d in range(4)]
    x_row = [lax.rem(at, 2) for at in x_at]
    x_col = [at // 2 * 8 for at in x_at]
    everyone = [(z_at[dz] + x_row[dx], x_col[dx] + y_at[dy] + core_at[dc]) for dz, dy, dx, dc in farthest_first(
        [(dz, dy, dx, dc) for dz in range(4) for dy in range(4) for dx in range(4) for dc in (0, 1)])]

    def tell(peers):
        for peer in peers:
            send(e_slot.at[pl.ds(me, 1)], e_slot.at[pl.ds(me, 1)], peer, 4)

    tell(everyone[:FAR])
    for to_row, to_col in row_peers:
        send(q_buf.at[:, window(to_col)], d_slot.at[col], (to_row, to_col), 3)
    tell(everyone[FAR:])

    await_bytes(d_slot, cols_n - 1, recv_sem.at[3])
    w2 = d_slot[0]
    for i in range(1, cols_n):
        w2 = w2 + d_slot[i]
    own_w2 = jnp.where(mine, w2, 0.0) + own_b[3:4] * own_w1
    own_b, own_w1, own_w2 = (
        jnp.where(odd == 1, pltpu.roll(value, modes, 1), value)[:, :modes] for value in (own_b, own_w1, own_w2))

    n = rows_n * cols_n
    await_bytes(e_slot, n - 1, recv_sem.at[4])
    line = jnp.sum(e_slot[...], axis=0, keepdims=True)
    g = jnp.concatenate([line, pltpu.roll(line, LANES - 4, 1), pltpu.roll(line, LANES - 8, 1), line], axis=0)
    g0, g1, g2, g3 = (g[:, i:i + 1] for i in range(4))
    a0 = g0 / g1
    norm = g0 - 2.0 * a0 * g1 + a0 * a0 * g2
    beta = norm / g0
    more = 1.0 + beta
    a1 = norm / (more * more * g1 - 2.0 * more * a0 * g2 + a0 * a0 * g3)
    r1 = own_b - a0 * own_w1
    results = [a0 * own_b + a1 * (r1 + beta * own_b) - r1, r1, a1 * (more * own_w1 - a0 * own_w2)]
    for ref, value in zip((x_part, res_part, res_step), results):
        ref[...] = value[0:3]

    await_bytes(a_slot, cols_n - 1, send_sem.at[0])
    await_bytes(p_slot, rows_n - 1, send_sem.at[1])
    await_bytes(d_slot, cols_n - 1, send_sem.at[3])
    await_bytes(e_slot, n - 1, send_sem.at[4])

    await_bytes(f_slot, 2, send_sem.at[2])


def solution(mesh):
    rows_n, cols_n = mesh.shape["row"], mesh.shape["col"]
    n = rows_n * cols_n

    def body(right_side, linewidth, scattering):
        block_rows, block_cols = scattering.shape
        vmem, anywhere = pl.BlockSpec(memory_space=pltpu.VMEM), pl.BlockSpec(memory_space=pl.ANY)
        line = linewidth.reshape(1, -1)
        x_part, res_part, res_step = pl.pallas_call(
            functools.partial(kernel, rows_n, cols_n),
            out_shape=(pltpu.VMEM(right_side.shape, F32),) * 3,
            in_specs=[anywhere] * 3,
            out_specs=(vmem,) * 3,
            scratch_shapes=[
                pltpu.VMEM((block_rows, block_cols), F32),
                pltpu.VMEM((block_rows, block_cols), BF16),
                pltpu.VMEM((block_rows, block_cols), BF16),
                pltpu.VMEM((block_cols, block_rows // 8 * TURNED), BF16),
                pltpu.VMEM((block_cols, block_rows // 8 * TURNED), BF16),
                pltpu.VMEM(right_side.shape, F32),
                pltpu.VMEM(line.shape, F32),
                pltpu.VMEM((cols_n, 4, PAD), F32),
                pltpu.VMEM((4, block_rows), F32),
                pltpu.VMEM((rows_n, 4, block_cols), F32),
                pltpu.VMEM((4, block_cols), F32),
                pltpu.VMEM((2, 4, block_cols), F32),
                pltpu.VMEM((4, block_rows), F32),
                pltpu.VMEM((cols_n, 4, PAD), F32),
                pltpu.VMEM((n, LANES), F32),
                pltpu.SemaphoreType.DMA((cols_n // 2,)),
                pltpu.SemaphoreType.DMA((2,)),
                pltpu.SemaphoreType.DMA((cols_n,)),
                pltpu.SemaphoreType.DMA((5,)),
                pltpu.SemaphoreType.DMA((5,)),
            ],
            compiler_params=pltpu.CompilerParams(
                collective_id=0, has_side_effects=True, vmem_limit_bytes=60 << 20),
        )(right_side, line, scattering)
        return x_part + res_part, res_part - res_step

    return jax.shard_map(
        body,
        mesh=mesh,
        in_specs=(P(None, ROW_COL), P(ROW_COL), P("row", "col")),
        out_specs=(P(None, ROW_COL), P(None, ROW_COL)),
        check_vma=False,
    )
```
